256 devices in a mesh: row: 32 (over y, x, core), col: 8 (over z).
Axes of the slice: x: 4, y: 4, z: 8, core: 2. Of those that a mesh axis runs over, the one named last changes fastest.
Arguments:
- head_points: float32 [8, 2, 1024], P(None, None, 'row'), may hold values from 0 to 1
- tail_points: float32 [8, 32768], P(None, 'row'), may hold values from 0 to 1
- eval_points: float32 [8, 8192], P(None, 'col'), may hold values from 0 to 1
- length_scales: float32 [8], replicated, may hold values from 0.5 to 2
- head_factor: float32 [2, 1024, 2, 1024], P(None, 'row', None, 'col'), as said below
- tail_factor: float32 [32768, 2, 1024], P('row', None, 'col'), may hold values from -0.125 to 0.125
Outputs:
- head_solved: float32 [2, 1024, 8192], P(None, 'row', 'col')
- tail_rhs: float32 [32768, 8192], P('row', 'col')
The draws below stay inside these ranges and needn't reach their ends.
Inputs may be any that keep to these rules, and one draw needn't show every extreme that they name: head_factor[p, :, q, :] is zero for q > p; the blocks with p = q are lower triangular with a diagonal between 1 and 2.
All inputs are finite; a program needn't handle non-finite values.
Results may differ from the reference program's by a relative error of at most 0.00011.
Values sent between devices are 32-bit elements; how exact they have to be, the bound alone decides.
No kernel may reach another device: no remote copies, remote signals or barrier semaphores. Data moves between devices by JAX's collectives and lax.ppermute only.
A program may use at most 192 MiB of HBM per device.

```python
import math
import jax
import jax.numpy as jnp
from jax import lax

PB = 1024
DIMS = 8
TRAIL = 32768
M = 8192


def draw_head_factor(key, part):
    key_noise = jax.random.fold_in(key, 11)
    key_diag = jax.random.fold_in(key, 23)
    noise = jax.random.normal(key_noise, (2, PB, 2, PB), jnp.float32)
    diagonal = jax.random.uniform(key_diag, (2, PB), jnp.float32, 1.0, 2.0)
    places = jnp.arange(PB)
    lower = (places[:, None] > places[None, :]).astype(jnp.float32)
    panels = jnp.arange(2)
    same = (panels[:, None] == panels[None, :]).astype(jnp.float32)
    below = (panels[:, None] > panels[None, :]).astype(jnp.float32)
    within = same[:, None, :, None] * lower[None, :, None, :] * (0.4 / PB ** 0.5)
    across = below[:, None, :, None] * jnp.ones((1, PB, 1, PB), jnp.float32) * (1.0 / PB ** 0.5)
    identity = same[:, None, :, None] * jnp.eye(PB, dtype=jnp.float32)[None, :, None, :]
    return noise * (within + across) + identity * diagonal[:, :, None, None]


def level_of(key, extent, shards, low, largest):
    loudness = 1.0
    for dim, parts in shards:
        draws = jax.random.uniform(jax.random.fold_in(jax.random.fold_in(key, 6), dim), (parts,), jnp.float32, low / len(shards), largest / len(shards))
        loudness = loudness * jnp.repeat(jnp.exp(draws), extent[dim] // parts).reshape((-1,) + (1,) * (len(extent) - 1 - dim))
    return loudness


def bell_draw(key, extent, width, limit, cuts=(), kind=jnp.bfloat16):
    array = width * jax.random.normal(key, extent, jnp.float32)
    if cuts:
        array = array * level_of(key, extent, cuts, -0.22, 0.18)
    return jnp.clip(array, -limit, limit).astype(kind)


def setup_inputs(seed: int = 0) -> dict:
    key_of = jax.random.split(jax.random.key(seed), 7)
    head_points = jnp.clip(1.0 * jax.random.uniform(key_of[0], (DIMS, 2, PB), jnp.float32) ** level_of(key_of[0], (DIMS, 2, PB), ((2, 32),), -0.2, 0.2), 0.0, 1.0)
    tail_points = jnp.clip(1.0 * jax.random.uniform(key_of[1], (DIMS, TRAIL), jnp.float32) ** level_of(key_of[1], (DIMS, TRAIL), ((1, 32),), -0.2, 0.2), 0.0, 1.0)
    eval_points = jnp.clip(1.0 * jax.random.uniform(key_of[2], (DIMS, M), jnp.float32) ** level_of(key_of[2], (DIMS, M), ((1, 8),), -0.2, 0.2), 0.0, 1.0)
    length_scales = jnp.clip(jnp.exp(jax.random.uniform(key_of[3], (DIMS,), jnp.float32, math.log(0.5), math.log(2.0))), 0.5, 2.0)
    head_factor = draw_head_factor(jax.random.fold_in(key_of[6], 71), 0)
    tail_factor = bell_draw(key_of[5], (TRAIL, 2, PB), (2 * PB) ** -0.5, 0.125, ((0, 32), (2, 8)), jnp.float32)
    return {"head_points": head_points, "tail_points": tail_points, "eval_points": eval_points, "length_scales": length_scales, "head_factor": head_factor, "tail_factor": tail_factor}


def kernel_block(row_points, col_points, length_scales):
    total = jnp.zeros((row_points.shape[1], col_points.shape[1]), jnp.float32)
    for dimension in range(DIMS):
        spread = (row_points[dimension][:, None] - col_points[dimension][None, :]) / length_scales[dimension]
        total = total + spread * spread
    scaled = jnp.sqrt(5.0 * total)
    return (1.0 + scaled + scaled * scaled / 3.0) * jnp.exp(-scaled)

def product(left, right):
    return jnp.dot(left.astype(jnp.float32), right.astype(jnp.float32), precision=lax.Precision.HIGHEST, preferred_element_type=jnp.float32)

def reference(head_points, tail_points, eval_points, length_scales, head_factor, tail_factor):
    first = kernel_block(head_points[:, 0, :], eval_points, length_scales)
    second = kernel_block(head_points[:, 1, :], eval_points, length_scales)
    tail = kernel_block(tail_points, eval_points, length_scales)
    solved_one = jax.scipy.linalg.solve_triangular(head_factor[0, :, 0, :], first, lower=True)
    second_rhs = second - product(head_factor[1, :, 0, :], solved_one)
    solved_two = jax.scipy.linalg.solve_triangular(head_factor[1, :, 1, :], second_rhs, lower=True)
    tail = tail - product(tail_factor[:, 0, :], solved_one)
    tail = tail - product(tail_factor[:, 1, :], solved_two)
    return (jnp.stack([solved_one, solved_two]), tail)
```

```python
import jax
import jax.numpy as jnp
from jax import lax
from jax.experimental import pallas as pl
from jax.experimental.pallas import tpu as pltpu
from jax.sharding import PartitionSpec as P

F32, BF16 = jnp.float32, jnp.bfloat16
PB, NE = 1024, 1024
CUT = 768
OFFSETS = (0, -1, 1, 2)
SHARD = 8 * 96 + 64


def split2(v):
    hi = v.astype(BF16)
    return hi, (v - hi.astype(F32)).astype(BF16)


def split3(v):
    a = v.astype(BF16)
    rest = v - a.astype(F32)
    b = rest.astype(BF16)
    return a, b, (rest - b.astype(F32)).astype(BF16)


def mm(a, b):
    return jnp.dot(a, b, preferred_element_type=F32)


def mm3(a, b):
    return mm(a[0], b[0]) + (mm(a[0], b[1]) + mm(a[1], b[0]))


def mmf(a, b):
    return jnp.dot(a, b, precision=lax.Precision.HIGHEST, preferred_element_type=F32)


def left_features(f):
    a, b, c = split3(f)
    group = lax.broadcasted_iota(jnp.int32, f.shape, 1) // 16
    a, b, c = a.astype(F32), b.astype(F32), c.astype(F32)
    picked = jnp.where((group == 2) | (group == 4), b, jnp.where(group == 5, c, a))
    return picked.astype(BF16)


def right_features(g):
    a, b, c = split3(g)
    none = jnp.zeros((32, g.shape[1]), BF16)
    return jnp.concatenate([a, b, a, c, b, a, none], 0)


def matern(left, right):
    total = jnp.maximum(mm(left, right), 0.0)
    scaled = jnp.sqrt(total)
    return (1.0 + scaled + total * (1.0 / 3.0)) * jnp.exp(-scaled)


def invert_own_kernel(where_ref, tiles_ref, out_ref):
    r, z = where_ref[0], where_ref[1]
    start = (r % 4) * 32
    mine = z == r // 4
    row = lax.broadcasted_iota(jnp.int32, (32, 128), 0)
    lane = lax.broadcasted_iota(jnp.int32, (32, 128), 1)
    inside = (lane >= start) & (lane < start + 32) & mine
    work = []
    for part in (0, 2):
        tile = tiles_ref[part * 32 : part * 32 + 32, :]
        block = pltpu.roll(tile, (128 - start) % 128, 1)
        diagonal = jnp.sum(jnp.where(lane == row, block, 0.0), axis=1, keepdims=True)
        scale = 1.0 / diagonal
        work.append([tile, block * scale, jnp.where(lane == row, scale, 0.0)])
    for k in range(31):
        for item in work:
            below = jnp.where(row > k, item[1][:, k : k + 1], 0.0)
            item[2] = item[2] - below * item[2][k : k + 1, :]
    for part, (tile, _, x) in zip((0, 2), work):
        out_ref[part * 32 : part * 32 + 32, :] = jnp.where(inside, pltpu.roll(x, start, 1), tile)
    out_ref[32:64, :] = tiles_ref[32:64, :]


def invert_own(where, tiles):
    return pl.pallas_call(
        invert_own_kernel,
        out_shape=jax.ShapeDtypeStruct((96, 128), F32),
        in_specs=[pl.BlockSpec(memory_space=pltpu.SMEM), pl.BlockSpec(memory_space=pltpu.VMEM)],
        out_specs=pl.BlockSpec(memory_space=pltpu.VMEM),
        cost_estimate=pl.CostEstimate(flops=1 << 20, bytes_accessed=1 << 17, transcendentals=0),
        name="invert_own",
    )(where, tiles)


def block_inverses(factor):
    row = lax.broadcasted_iota(jnp.int32, (256, 256), 0)
    column = lax.broadcasted_iota(jnp.int32, (256, 256), 1)
    whole = [
        jnp.concatenate([factor[2 * i, i * 256 : i * 256 + 256, :], factor[2 * i + 1, i * 256 : i * 256 + 256, :]], 1)
        for i in range(4)
    ]
    inverse = [jnp.where(row // 32 == column // 32, w, 0.0) for w in whole]
    for size in (32, 64, 128):
        below = (row // (2 * size) == column // (2 * size)) & (row // size % 2 == 1) & (column // size % 2 == 0)
        inner = [mmf(jnp.where(below, w, 0.0), d) for w, d in zip(whole, inverse)]
        inverse = [d - mmf(d, t) for d, t in zip(inverse, inner)]
    return inverse


def solve_kernel(where_ref, *refs):
    pieces, (g_ref, head_ref, hi_ref, lo_ref, factor_ref, points_ref, solved_ref) = refs[:8], refs[8:]
    r = where_ref[0]
    y, x, core = r // 8, (r // 2) % 4, r % 2
    for other in range(2):
        source = (core + other) % 2
        for k in range(4):
            for m in range(4):
                first, second = OFFSETS[m], OFFSETS[k]
                yy = (y + 4 + jnp.where(source == 0, second, first)) % 4
                xx = (x + 4 + jnp.where(source == 0, first, second)) % 4
                row = pl.multiple_of(32 * ((yy * 4 + xx) * 2 + source), 32)
                piece = pieces[other * 4 + k]
                for z in range(8):
                    for part in range(3):
                        at = z * 96 + part * 32
                        factor_ref[part, z, pl.ds(row, 32), :] = piece[m, at : at + 32, :]
                for panel in range(2):
                    at = 768 + panel * 32
                    points_ref[panel, pl.ds(row, 32), :] = piece[m, at : at + 32, :]
    right = right_features(g_ref[...])
    for panel in range(2):
        inverse = block_inverses(factor_ref.at[2 * panel])
        for i in range(4):
            rows = slice(i * 256, i * 256 + 256)
            total = matern(left_features(points_ref[panel, rows, :]), right)
            blocks = [(1, j, 0) for j in range(4)] if panel else []
            blocks += [(2 * panel, j, panel) for j in range(i)]
            for part, j, of in blocks:
                left = jnp.concatenate([factor_ref[part, 2 * j, rows, :], factor_ref[part, 2 * j + 1, rows, :]], 1)
                at = [slice((2 * j + h) * 256 + of * 128, (2 * j + h) * 256 + of * 128 + 128) for h in range(2)]
                known = [jnp.concatenate([ref[at[0], :], ref[at[1], :]], 0) for ref in (hi_ref, lo_ref)]
                total = total - mm3(split2(left), known)
            solved = mm3(split2(inverse[i]), split2(total))
            solved_ref[panel, rows, :] = solved
            hi, lo = split2(solved)
            for h in range(2):
                at = slice((2 * i + h) * 256 + panel * 128, (2 * i + h) * 256 + panel * 128 + 128)
                hi_ref[at, :] = hi[h * 128 : h * 128 + 128, :]
                lo_ref[at, :] = lo[h * 128 : h * 128 + 128, :]
    own = pl.multiple_of(r * 32, 32)
    for panel in range(2):
        head_ref[panel] = solved_ref[panel, pl.ds(own, 32), :]


def solve(where, pieces, g):
    vmem = pl.BlockSpec(memory_space=pltpu.VMEM)
    return pl.pallas_call(
        solve_kernel,
        out_shape=(
            jax.ShapeDtypeStruct((2, 32, NE), F32),
            jax.ShapeDtypeStruct((2 * PB, NE), BF16),
            jax.ShapeDtypeStruct((2 * PB, NE), BF16),
        ),
        in_specs=[pl.BlockSpec(memory_space=pltpu.SMEM)] + [vmem] * 9,
        out_specs=(vmem, vmem, vmem),
        scratch_shapes=[
            pltpu.VMEM((3, 8, PB, 128), F32),
            pltpu.VMEM((2, PB, 128), F32),
            pltpu.VMEM((2, PB, NE), F32),
        ],
        compiler_params=pltpu.CompilerParams(vmem_limit_bytes=60 << 20),
        cost_estimate=pl.CostEstimate(flops=15 << 30, bytes_accessed=24 << 20, transcendentals=4 << 20),
        name="solve_panels",
    )(where, *pieces, g)


def update_kernel(f_ref, g_ref, a_ref, hi_ref, lo_ref, *rest):
    out_ref = rest[-1]
    total = matern(left_features(f_ref[...]), right_features(g_ref[...]))
    n = f_ref.shape[0]
    left = []
    for z in range(8):
        left += [a_ref[z, pl.ds(q, n, stride=2), :] for q in range(2)]
    hi, lo = split2(jnp.concatenate(left, 1))
    out_ref[...] = total - mm3((hi, lo), (hi_ref[...], lo_ref[...]))


def update(f, g, a, hi, lo, start, out=None):
    step = 256
    count = a.shape[1] // (2 * step)
    first = start // step
    whole = lambda i: (0, 0)
    in_specs = [
        pl.BlockSpec((step, 128), lambda i: (i + first, 0)),
        pl.BlockSpec((16, NE), whole),
        pl.BlockSpec((8, 2 * step, 128), lambda i: (0, i, 0)),
        pl.BlockSpec((2 * PB, NE), whole, pipeline_mode=pl.Buffered(1)),
        pl.BlockSpec((2 * PB, NE), whole, pipeline_mode=pl.Buffered(1)),
    ]
    args = [f, g, a, hi, lo]
    aliases = {}
    if out is not None:
        in_specs.append(pl.BlockSpec(memory_space=pl.ANY))
        args.append(out)
        aliases = {5: 0}
    return pl.pallas_call(
        update_kernel,
        grid=(count,),
        out_shape=jax.ShapeDtypeStruct((1024, NE), F32),
        in_specs=in_specs,
        out_specs=pl.BlockSpec((step, NE), lambda i: (i + first, 0)),
        input_output_aliases=aliases,
        compiler_params=pltpu.CompilerParams(vmem_limit_bytes=48 << 20),
        cost_estimate=pl.CostEstimate(
            flops=count * step * 2 * PB * NE * 6, bytes_accessed=12 << 20, transcendentals=count << 18
        ),
        name="update_tail",
    )(*args)


def hop(v, phase, shift):
    moves = []
    for r in range(32):
        y, x, core = r // 8, (r // 2) % 4, r % 2
        if (core + phase) % 2 == 0:
            x = (x + shift) % 4
        else:
            y = (y + shift) % 4
        moves.append((r, (y * 4 + x) * 2 + core))
    return lax.ppermute(v, "row", moves)


def gather_four(v, phase, cut):
    from_before, from_after = hop(v, phase, 1), hop(v, phase, -1)
    two_before = hop(from_before[:cut], phase, 1)
    two_after = hop(from_after[cut:], phase, -1)
    return [v, from_before, from_after, jnp.concatenate([two_before, two_after], 0)]


def row_features(points, scale):
    u = ((points - 0.5) * scale).T
    n = u.shape[0]
    norm = jnp.sum(u * u, axis=1, keepdims=True)
    f = jnp.concatenate([u, norm, jnp.ones((n, 1), F32), jnp.zeros((n, 6), F32)], 1)
    return jnp.concatenate([f] * 6 + [jnp.zeros((n, 32), F32)], 1)


def column_features(points, scale):
    v = (points - 0.5) * scale
    n = v.shape[1]
    norm = jnp.sum(v * v, axis=0, keepdims=True)
    return jnp.concatenate([-2.0 * v, jnp.ones((1, n), F32), norm, jnp.zeros((6, n), F32)], 0)


def per_device(head_points, tail_points, eval_points, length_scales, head_factor, tail_factor):
    where = jnp.stack([lax.axis_index("row"), lax.axis_index("col")]).astype(jnp.int32)
    rows_one = lax.all_gather(tail_factor[:CUT], "col", axis=0, tiled=False)
    rows_two = lax.all_gather(tail_factor[CUT:], "col", axis=0, tiled=False)

    scale = (5.0**0.5 / length_scales)[:, None]
    tiles = jnp.concatenate([head_factor[0, :, 0], head_factor[1, :, 0], head_factor[1, :, 1]], 0)
    tiles = invert_own(where, tiles)
    spread = lax.all_to_all(jnp.broadcast_to(tiles[None], (8, 96, 128)), "col", 0, 0)
    points = row_features(head_points.reshape(8, 64), scale)
    shard = jnp.concatenate([spread.reshape(768, 128), points], 0)

    line = jnp.stack(gather_four(shard, 0, SHARD // 2))
    plane = gather_four(line, 1, 2)
    pieces = plane + [lax.ppermute(v, "row", [(r, r ^ 1) for r in range(32)]) for v in plane]

    g = column_features(eval_points, scale)
    head, hi, lo = solve(where, pieces, g)
    f = row_features(tail_points, scale)
    tail = update(f, g, rows_one.reshape(8, 2 * CUT, 128), hi, lo, 0)
    tail = update(f, g, rows_two.reshape(8, 2 * (1024 - CUT), 128), hi, lo, CUT, tail)
    return head, tail


def solution(mesh):
    placed = (
        P(None, None, "row"),
        P(None, "row"),
        P(None, "col"),
        P(),
        P(None, "row", None, "col"),
        P("row", None, "col"),
    )
    return jax.shard_map(
        per_device,
        mesh=mesh,
        in_specs=placed,
        out_specs=(P(None, "row", "col"), P("row", "col")),
        check_vma=False,
    )
```

```python
import jax
import jax.numpy as jnp
from jax import lax
from jax.experimental import pallas as pl
from jax.experimental.pallas import tpu as pltpu
from jax.sharding import PartitionSpec as P

F32, BF16 = jnp.float32, jnp.bfloat16
PB, NE = 1024, 1024
HALVES = 2
OFFSETS = (0, -1, 1, 2)
SHARD = 3 * 8 * 32 + 8


def split2(v):
    hi = v.astype(BF16)
    return hi, (v - hi.astype(F32)).astype(BF16)


def split3(v):
    a = v.astype(BF16)
    rest = v - a.astype(F32)
    b = rest.astype(BF16)
    return a, b, (rest - b.astype(F32)).astype(BF16)


def mm(a, b):
    return jnp.dot(a, b, preferred_element_type=F32)


def mm3(a, b):
    return mm(a[0], b[0]) + (mm(a[0], b[1]) + mm(a[1], b[0]))


def features(points, scale, right):
    u = (points - 0.5) * scale
    n = u.shape[1]
    norm = jnp.sum(u * u, axis=0, keepdims=True)
    one, none = jnp.ones((1, n), F32), jnp.zeros((6, n), F32)
    rest = jnp.zeros((32, n), BF16)
    if right:
        a, b, c = split3(jnp.concatenate([-2.0 * u, one, norm, none], 0))
        return jnp.concatenate([a, b, a, c, b, a, rest], 0)
    a, b, c = split3(jnp.concatenate([u, norm, one, none], 0))
    return jnp.concatenate([a, a, b, a, b, c, rest], 0)


def matern(left, right):
    total = lax.dot_general(left, right, (((0,), (0,)), ((), ())), preferred_element_type=F32)
    total = jnp.maximum(total, 0.0)
    scaled = jnp.sqrt(total)
    return (1.0 + scaled + total * (1.0 / 3.0)) * jnp.exp(-scaled)


def invert_own_kernel(tiles_ref, out_ref):
    r, z = lax.axis_index("row"), lax.axis_index("col")
    start = (r % 4) * 32
    mine = z == r // 4
    row = lax.broadcasted_iota(jnp.int32, (32, 128), 0)
    lane = lax.broadcasted_iota(jnp.int32, (32, 128), 1)
    inside = (lane >= start) & (lane < start + 32) & mine
    work = []
    for panel in range(2):
        tile = tiles_ref[panel, pl.ds(panel, 32, stride=2), :]
        block = pltpu.roll(tile, (128 - start) % 128, 1)
        diagonal = jnp.sum(jnp.where(lane == row, block, 0.0), axis=1, keepdims=True)
        scale = 1.0 / diagonal
        work.append([tile, block * scale, jnp.where(lane == row, scale, 0.0)])
    for k in range(31):
        for item in work:
            below = jnp.where(row > k, item[1][:, k : k + 1], 0.0)
            item[2] = item[2] - below * item[2][k : k + 1, :]
    done = [jnp.where(inside, pltpu.roll(x, start, 1), tile) for tile, _, x in work]
    for copy in range(8):
        out_ref[copy, 0:32, :] = done[0]
        out_ref[copy, 32:64, :] = tiles_ref[1, pl.ds(0, 32, stride=2), :]
        out_ref[copy, 64:96, :] = done[1]


def invert_own(tiles):
    vmem = pl.BlockSpec(memory_space=pltpu.VMEM)
    return pl.pallas_call(
        invert_own_kernel,
        out_shape=jax.ShapeDtypeStruct((8, 96, 128), F32),
        in_specs=[vmem],
        out_specs=vmem,
        cost_estimate=pl.CostEstimate(flops=1 << 20, bytes_accessed=1 << 19, transcendentals=0),
        name="invert_own",
    )(tiles)


def block_inverses(factor):
    row = lax.broadcasted_iota(jnp.int32, (256, 256), 0)
    column = lax.broadcasted_iota(jnp.int32, (256, 256), 1)
    whole = [
        jnp.concatenate([factor[2 * i, i * 256 : i * 256 + 256, :], factor[2 * i + 1, i * 256 : i * 256 + 256, :]], 1)
        for i in range(4)
    ]
    inverse = [jnp.where(row // 32 == column // 32, w, 0.0) for w in whole]
    for size in (32, 64, 128):
        below = (row // (2 * size) == column // (2 * size)) & (row // size % 2 == 1) & (column // size % 2 == 0)
        inner = [mm3(split2(jnp.where(below, w, 0.0)), split2(d)) for w, d in zip(whole, inverse)]
        inverse = [d - mm3(split2(d), split2(t)) for d, t in zip(inverse, inner)]
    return inverse


def solve_kernel(*refs):
    pieces, (scale_ref, eval_ref, head_ref, hi_out, lo_out) = refs[:10], refs[10:15]
    stage_ref, factor_ref, solved_ref, hi_ref, lo_ref, sems, out_sems = refs[15:]
    r = lax.axis_index("row")
    y, x, core = r // 8, (r // 2) % 4, r % 2
    early, late = [], []
    for n, piece in enumerate(pieces):
        at = stage_ref.at[n // 5, min(n % 5, 3)]
        if n % 5 >= 3:
            at = at.at[(n % 5 - 3) * 2 : (n % 5 - 3) * 2 + 2]
        early.append(pltpu.make_async_copy(piece.at[:, 0:264], at.at[:, 0:264], sems.at[0, n]))
        late.append(pltpu.make_async_copy(piece.at[:, 264:SHARD], at.at[:, 264:SHARD], sems.at[1, n]))
    for copy in early + late:
        copy.start()
    sources = []
    for other in range(2):
        source = (core + other) % 2
        for k in range(4):
            for m in range(4):
                first, second = OFFSETS[m], OFFSETS[k]
                yy = (y + 4 + jnp.where(source == 0, second, first)) % 4
                xx = (x + 4 + jnp.where(source == 0, first, second)) % 4
                sources.append((stage_ref.at[other, k, m], pl.multiple_of(32 * ((yy * 4 + xx) * 2 + source), 32)))
    right = features(eval_ref[...], scale_ref[...], True)

    def place(part, at):
        for stage, row in sources:
            for z in range(8):
                factor_ref[part, z, pl.ds(row, 32), :] = stage[at + z * 32 : at + z * 32 + 32, :]

    for copy in early:
        copy.wait()
    place(0, 8)
    for panel in range(2):
        for n in range(0, 32, 8):
            points = jnp.concatenate([s[0:8, panel * 32 : panel * 32 + 32] for s, _ in sources[n : n + 8]], 1)
            values = matern(features(points, scale_ref[...], False), right)
            for j, (_, row) in enumerate(sources[n : n + 8]):
                solved_ref[panel, pl.ds(row, 32), :] = values[j * 32 : j * 32 + 32, :]

    out = []
    for panel in range(2):
        if panel == 1:
            for copy in late:
                copy.wait()
            place(1, 264)
            place(2, 520)
        inverse = [split2(v) for v in block_inverses(factor_ref.at[2 * panel])]
        for i in range(4):
            rows = slice(i * 256, i * 256 + 256)
            left = [factor_ref[1, z, rows, :] for z in range(8)] if panel else []
            left += [factor_ref[2 * panel, z, rows, :] for z in range(2 * i)]
            at = panel * PB + i * 256
            left = split2(jnp.concatenate(left, 1)) if left else None
            for half in range(HALVES):
                cols = slice(half * NE // HALVES, (half + 1) * NE // HALVES)
                total = solved_ref[panel, rows, cols]
                if left is not None:
                    total = total - mm3(left, (hi_ref[0:at, cols], lo_ref[0:at, cols]))
                solved = mm3(inverse[i], split2(total))
                solved_ref[panel, rows, cols] = solved
                hi_ref[at : at + 256, cols], lo_ref[at : at + 256, cols] = split2(solved)
            for n, (ref, whole) in enumerate(((hi_ref, hi_out), (lo_ref, lo_out))):
                sem = out_sems.at[n, panel * 4 + i]
                out.append(pltpu.make_async_copy(ref.at[at : at + 256], whole.at[at : at + 256], sem))
                out[-1].start()
    own = pl.multiple_of(r * 32, 32)
    for panel in range(2):
        head_ref[panel] = solved_ref[panel, pl.ds(own, 32), :]
    for copy in out:
        copy.wait()


def solve(pieces, scale, evals):
    vmem, whole = pl.BlockSpec(memory_space=pltpu.VMEM), pl.BlockSpec(memory_space=pl.ANY)
    return pl.pallas_call(
        solve_kernel,
        out_shape=(
            jax.ShapeDtypeStruct((2, 32, NE), F32),
            jax.ShapeDtypeStruct((2 * PB, NE), BF16),
            jax.ShapeDtypeStruct((2 * PB, NE), BF16),
        ),
        in_specs=[whole] * 10 + [vmem] * 2,
        out_specs=(vmem, whole, whole),
        scratch_shapes=[
            pltpu.VMEM((2, 4, 4, SHARD, 128), F32),
            pltpu.VMEM((3, 8, PB, 128), F32),
            pltpu.VMEM((2, PB, NE), F32),
            pltpu.VMEM((2 * PB, NE), BF16),
            pltpu.VMEM((2 * PB, NE), BF16),
            pltpu.SemaphoreType.DMA((2, 10)),
            pltpu.SemaphoreType.DMA((2, 8)),
        ],
        compiler_params=pltpu.CompilerParams(vmem_limit_bytes=54 << 20),
        cost_estimate=pl.CostEstimate(flops=15 << 30, bytes_accessed=16 << 20, transcendentals=4 << 20),
        name="solve_panels",
    )(*pieces, scale, evals)


def tail_kernel(points_ref, eval_ref, scale_ref, out_ref):
    right = features(eval_ref[...], scale_ref[...], True)
    out_ref[...] = matern(features(points_ref[...], scale_ref[...], False), right)


def tail_block(points, evals, scale):
    vmem = pl.BlockSpec(memory_space=pltpu.VMEM)
    return pl.pallas_call(
        tail_kernel,
        grid=(4,),
        out_shape=jax.ShapeDtypeStruct((1024, NE), F32),
        in_specs=[pl.BlockSpec((8, 256), lambda i: (0, i)), vmem, vmem],
        out_specs=pl.BlockSpec((256, NE), lambda i: (i, 0)),
        cost_estimate=pl.CostEstimate(flops=1 << 28, bytes_accessed=4 << 20, transcendentals=2 << 20),
        name="tail_block",
    )(points, evals, scale)


def update_kernel(tail_in, a_in, hi_in, lo_in, out_ref, a_ref, hi_ref, lo_ref, rows_ref, sems, out_sems):
    fetches = []

    def fetch(source, target):
        copy = pltpu.make_async_copy(source, target, sems.at[len(fetches)])
        copy.start()
        fetches.append(copy)
        return copy

    def rows(b):
        return slice(b * 256, b * 256 + 256)

    def part(b):
        return [fetch(a_in.at[:, :, rows(b)], a_ref.at[:, :, rows(b)]), fetch(tail_in.at[rows(b)], rows_ref.at[rows(b)])]

    def known(q):
        at = slice(q * PB, q * PB + PB)
        return [fetch(i.at[at], o.at[at]) for i, o in ((hi_in, hi_ref), (lo_in, lo_ref))]

    arrive = [part(0)]
    solved = [known(0), known(1)]
    arrive += [part(b) for b in range(1, 4)]
    out = []
    for b in range(4):
        for copy in arrive[b]:
            copy.wait()
        for q in range(2):
            if b == 0:
                for copy in solved[q]:
                    copy.wait()
            left = jnp.concatenate([a_ref[z, q, rows(b), :] for z in range(8)], 1)
            at = slice(q * PB, q * PB + PB)
            rows_ref[rows(b)] = rows_ref[rows(b)] - mm3(split2(left), (hi_ref[at, :], lo_ref[at, :]))
        out.append(pltpu.make_async_copy(rows_ref.at[rows(b)], out_ref.at[rows(b)], out_sems.at[b]))
        out[b].start()
    for copy in out:
        copy.wait()


def update(tail, a, hi, lo):
    whole = pl.BlockSpec(memory_space=pl.ANY)
    return pl.pallas_call(
        update_kernel,
        out_shape=jax.ShapeDtypeStruct((1024, NE), F32),
        in_specs=[whole] * 4,
        out_specs=whole,
        scratch_shapes=[
            pltpu.VMEM((8, 2, 1024, 128), F32),
            pltpu.VMEM((2 * PB, NE), BF16),
            pltpu.VMEM((2 * PB, NE), BF16),
            pltpu.VMEM((1024, NE), F32),
            pltpu.SemaphoreType.DMA((12,)),
            pltpu.SemaphoreType.DMA((4,)),
        ],
        compiler_params=pltpu.CompilerParams(vmem_limit_bytes=58 << 20),
        cost_estimate=pl.CostEstimate(flops=12 << 30, bytes_accessed=24 << 20, transcendentals=0),
        name="update_tail",
    )(tail, a, hi, lo)


def hop(v, phase, shift):
    moves = []
    for r in range(32):
        y, x, core = r // 8, (r // 2) % 4, r % 2
        if (core + phase) % 2 == 0:
            x = (x + shift) % 4
        else:
            y = (y + shift) % 4
        moves.append((r, (y * 4 + x) * 2 + core))
    return lax.ppermute(v, "row", moves)


def gather_four(v, phase, cut):
    from_before, from_after = hop(v, phase, 1), hop(v, phase, -1)
    two_before = hop(from_before[:cut], phase, 1)
    two_after = hop(from_after[cut:], phase, -1)
    return [v, from_before, from_after, two_before, two_after]


def per_device(head_points, tail_points, eval_points, length_scales, head_factor, tail_factor):
    scale = (5.0**0.5 / length_scales)[:, None]
    tiles = invert_own(head_factor.reshape(2, 64, 128))
    spread = lax.all_to_all(tiles, "col", 0, 0)
    tail = tail_block(tail_points, eval_points, scale)
    spread, tail, tail_factor = lax.optimization_barrier((spread, tail, tail_factor.transpose(1, 0, 2)))
    tail_rows = lax.all_gather(tail_factor, "col", axis=0, tiled=False)
    points = jnp.pad(head_points.reshape(8, 64), ((0, 0), (0, 64)))
    spread = spread.reshape(8, 3, 32, 128).transpose(1, 0, 2, 3).reshape(768, 128)
    shard = jnp.concatenate([points, spread], 0)

    line = gather_four(shard, 0, SHARD // 2 // 8 * 8)
    line = jnp.stack(line[:3] + [jnp.concatenate(line[3:], 0)])
    plane = gather_four(line, 1, 2)
    pieces = plane + [lax.ppermute(v, "row", [(r, r ^ 1) for r in range(32)]) for v in plane]

    head, hi, lo = solve(pieces, scale, eval_points)
    tail = update(tail, tail_rows, hi, lo)
    return head, tail


def solution(mesh):
    placed = (
        P(None, None, "row"),
        P(None, "row"),
        P(None, "col"),
        P(),
        P(None, "row", None, "col"),
        P("row", None, "col"),
    )
    return jax.shard_map(
        per_device,
        mesh=mesh,
        in_specs=placed,
        out_specs=(P(None, "row", "col"), P("row", "col")),
        check_vma=False,
    )
```

```python
import jax
import jax.numpy as jnp
from jax import lax
from jax.experimental import pallas as pl
from jax.experimental.pallas import tpu as pltpu
from jax.sharding import PartitionSpec as P

F32, BF16 = jnp.float32, jnp.bfloat16
PB, NE = 1024, 1024
HALVES = 2
OFFSETS = (0, -1, 1, 2)


def split2(v):
    hi = v.astype(BF16)
    return hi, (v - hi.astype(F32)).astype(BF16)


def split3(v):
    a = v.astype(BF16)
    rest = v - a.astype(F32)
    b = rest.astype(BF16)
    return a, b, (rest - b.astype(F32)).astype(BF16)


def mm(a, b):
    return jnp.dot(a, b, preferred_element_type=F32)


def mm3(a, b):
    return mm(a[0], b[0]) + (mm(a[0], b[1]) + mm(a[1], b[0]))


def features(points, scale, right):
    u = (points - 0.5) * scale
    n = u.shape[1]
    norm = jnp.sum(u * u, axis=0, keepdims=True)
    one, none = jnp.ones((1, n), F32), jnp.zeros((6, n), F32)
    rest = jnp.zeros((32, n), BF16)
    if right:
        a, b, c = split3(jnp.concatenate([-2.0 * u, one, norm, none], 0))
        return jnp.concatenate([a, b, a, c, b, a, rest], 0)
    a, b, c = split3(jnp.concatenate([u, norm, one, none], 0))
    return jnp.concatenate([a, a, b, a, b, c, rest], 0)


def matern(left, right):
    total = lax.dot_general(left, right, (((0,), (0,)), ((), ())), preferred_element_type=F32)
    total = jnp.maximum(total, 0.0)
    scaled = jnp.sqrt(total)
    return (1.0 + scaled + total * (1.0 / 3.0)) * jnp.exp(-scaled)


def invert_own_kernel(tiles_ref, out_ref):
    r, z = lax.axis_index("row"), lax.axis_index("col")
    start = (r % 4) * 32
    mine = z == r // 4
    row = lax.broadcasted_iota(jnp.int32, (32, 128), 0)
    lane = lax.broadcasted_iota(jnp.int32, (32, 128), 1)
    inside = (lane >= start) & (lane < start + 32) & mine
    work = []
    for panel in range(2):
        tile = tiles_ref[panel, pl.ds(panel, 32, stride=2), :]
        block = pltpu.roll(tile, (128 - start) % 128, 1)
        diagonal = jnp.sum(jnp.where(lane == row, block, 0.0), axis=1, keepdims=True)
        scale = 1.0 / diagonal
        work.append([tile, block * scale, jnp.where(lane == row, scale, 0.0)])
    for k in range(31):
        for item in work:
            below = jnp.where(row > k, item[1][:, k : k + 1], 0.0)
            item[2] = item[2] - below * item[2][k : k + 1, :]
    done = [jnp.where(inside, pltpu.roll(x, start, 1), tile) for tile, _, x in work]
    out_ref[0] = done[0]
    out_ref[1] = tiles_ref[1, pl.ds(0, 32, stride=2), :]
    out_ref[2] = done[1]


def invert_own(tiles):
    vmem = pl.BlockSpec(memory_space=pltpu.VMEM)
    return pl.pallas_call(
        invert_own_kernel,
        out_shape=jax.ShapeDtypeStruct((3, 32, 128), F32),
        in_specs=[vmem],
        out_specs=vmem,
        cost_estimate=pl.CostEstimate(flops=1 << 20, bytes_accessed=1 << 17, transcendentals=0),
        name="invert_own",
    )(tiles)


def pack_kernel(points_ref, *refs):
    tiles, out_ref = refs[:8], refs[8]
    out_ref[8] = jnp.zeros((32, 128), F32)
    out_ref[8, 0:8, :] = points_ref[...]
    for part in range(3):
        for n, tile in enumerate(tiles):
            out_ref[part * 8 + n + (1 if part else 0)] = tile[part]


def pack(points, tiles):
    vmem = pl.BlockSpec(memory_space=pltpu.VMEM)
    return pl.pallas_call(
        pack_kernel,
        out_shape=jax.ShapeDtypeStruct((25, 32, 128), F32),
        in_specs=[vmem] * 9,
        out_specs=vmem,
        cost_estimate=pl.CostEstimate(flops=0, bytes_accessed=1 << 20, transcendentals=0),
        name="pack",
    )(points, *tiles)


def block_inverses(blocks):
    row = lax.broadcasted_iota(jnp.int32, (256, 256), 0)
    column = lax.broadcasted_iota(jnp.int32, (256, 256), 1)
    inverse = [jnp.where(row // 32 == column // 32, w, 0.0) for w in blocks]
    for size in (32, 64, 128):
        below = (row // (2 * size) == column // (2 * size)) & (row // size % 2 == 1) & (column // size % 2 == 0)
        inner = [mm3(split2(jnp.where(below, w, 0.0)), split2(d)) for w, d in zip(blocks, inverse)]
        inverse = [d - mm3(split2(d), split2(t)) for d, t in zip(inverse, inner)]
    return [split2(d) for d in inverse]


def source_row(other, k, m):
    r = lax.axis_index("row")
    y, x, source = r // 8, (r // 2) % 4, (r % 2 + other) % 2
    first, second = OFFSETS[m], OFFSETS[k]
    yy = (y + 4 + jnp.where(source == 0, second, first)) % 4
    xx = (x + 4 + jnp.where(source == 0, first, second)) % 4
    return pl.multiple_of(32 * ((yy * 4 + xx) * 2 + source), 32)


def entries(pieces):
    count = len(pieces) // 2
    for n, piece in enumerate(pieces):
        other, k = n // count, n % count
        for m in range(piece.shape[0]):
            yield piece, m, other, min(k, 3), m + (2 if k == 4 else 0)


def substitute(part, at, before, factor_ref, solved_ref, hi_ref, lo_ref, hi_out, lo_out, sems):
    z = lax.axis_index("col")

    def tiles(p, rows, count):
        return [factor_ref[p, (z + 8 - n) % 8, rows, :] for n in range(count)]

    blocks = [slice(i * 256, i * 256 + 256) for i in range(4)]
    inverse = block_inverses([jnp.concatenate(tiles(part, rows, 2 * i + 2)[2 * i :], 1) for i, rows in enumerate(blocks)])
    halves = [slice(h * NE // HALVES, (h + 1) * NE // HALVES) for h in range(HALVES)]
    out = []
    for i, rows in enumerate(blocks):
        left = [t for p in before for t in tiles(p, rows, 8)] + tiles(part, rows, 2 * i)
        total = [solved_ref[rows, cols] for cols in halves]
        here = at + i * 256
        if left:
            left = split2(jnp.concatenate(left, 1))
            total = [t - mm3(left, (hi_ref[0:here, cols], lo_ref[0:here, cols])) for t, cols in zip(total, halves)]
        total = [mm3(inverse[i], split2(t)) for t in total]
        for t, cols in zip(total, halves):
            solved_ref[rows, cols] = t
            hi_ref[here : here + 256, cols], lo_ref[here : here + 256, cols] = split2(t)
        for n, (ref, whole) in enumerate(((hi_ref, hi_out), (lo_ref, lo_out))):
            out.append(pltpu.make_async_copy(ref.at[here : here + 256], whole.at[rows], sems.at[n, i]))
            out[-1].start()
    return out


def solve_first_kernel(*refs):
    pieces, (scale_ref, eval_ref, head_ref, hi_out, lo_out, second_out) = refs[:8], refs[8:14]
    points_ref, factor_ref, solved_ref, second_ref, hi_ref, lo_ref, sems, out_sems = refs[14:]
    near = [pltpu.make_async_copy(p.at[:, 8, 0:8], points_ref.at[n], sems.at[n]) for n, p in enumerate(pieces)]
    for copy in near:
        copy.start()
    rows = []
    for piece, m, other, k, entry in entries(pieces):
        row = source_row(other, k, entry)
        rows.append(row)
        pltpu.make_async_copy(piece.at[m, 0:8], factor_ref.at[0, :, pl.ds(row, 32)], sems.at[8]).start()
    right = features(eval_ref[...], scale_ref[...], True)
    for copy in near:
        copy.wait()
    for panel, target in ((0, solved_ref), (1, second_ref)):
        for n in range(0, 32, 8):
            points = [points_ref[e // 4, e % 4, :, panel * 32 : panel * 32 + 32] for e in range(n, n + 8)]
            values = matern(features(jnp.concatenate(points, 1), scale_ref[...], False), right)
            for j in range(8):
                target[pl.ds(rows[n + j], 32), :] = values[j * 32 : j * 32 + 32, :]
    second = pltpu.make_async_copy(second_ref, second_out, sems.at[9])
    second.start()
    pltpu.make_async_copy(factor_ref, factor_ref, sems.at[8]).wait()
    out = substitute(0, 0, (), factor_ref, solved_ref, hi_ref, lo_ref, hi_out, lo_out, out_sems)
    head_ref[...] = solved_ref[pl.ds(pl.multiple_of(lax.axis_index("row") * 32, 32), 32), :]
    for copy in out:
        copy.wait()
    second.wait()


def solve_first(pieces, scale, evals):
    vmem, whole = pl.BlockSpec(memory_space=pltpu.VMEM), pl.BlockSpec(memory_space=pltpu.HBM)
    return pl.pallas_call(
        solve_first_kernel,
        out_shape=(
            jax.ShapeDtypeStruct((32, NE), F32),
            jax.ShapeDtypeStruct((PB, NE), BF16),
            jax.ShapeDtypeStruct((PB, NE), BF16),
            jax.ShapeDtypeStruct((PB, NE), F32),
        ),
        in_specs=[whole] * 8 + [vmem] * 2,
        out_specs=(vmem, whole, whole, whole),
        scratch_shapes=[
            pltpu.VMEM((8, 4, 8, 128), F32),
            pltpu.VMEM((1, 8, PB, 128), F32),
            pltpu.VMEM((PB, NE), F32),
            pltpu.VMEM((PB, NE), F32),
            pltpu.VMEM((PB, NE), BF16),
            pltpu.VMEM((PB, NE), BF16),
            pltpu.SemaphoreType.DMA((10,)),
            pltpu.SemaphoreType.DMA((2, 4)),
        ],
        compiler_params=pltpu.CompilerParams(vmem_limit_bytes=60 << 20),
        cost_estimate=pl.CostEstimate(flops=9 << 30, bytes_accessed=8 << 20, transcendentals=4 << 20),
        name="solve_first",
    )(*pieces, scale, evals)


def solve_second_kernel(*refs):
    pieces, (hi_in, lo_in, second_in, head_ref, hi_out, lo_out) = refs[:10], refs[10:16]
    factor_ref, solved_ref, hi_ref, lo_ref, sems, out_sems = refs[16:]
    for part in (1, 0):
        for piece, m, other, k, entry in entries(pieces):
            target = factor_ref.at[part, :, pl.ds(source_row(other, k, entry), 32)]
            pltpu.make_async_copy(piece.at[m, part * 8 : part * 8 + 8], target, sems.at[part]).start()
    known = [
        pltpu.make_async_copy(second_in, solved_ref, sems.at[2]),
        pltpu.make_async_copy(hi_in, hi_ref.at[0:PB], sems.at[3]),
        pltpu.make_async_copy(lo_in, lo_ref.at[0:PB], sems.at[4]),
    ]
    for copy in known:
        copy.start()
    for part in (1, 0):
        pltpu.make_async_copy(factor_ref.at[part], factor_ref.at[part], sems.at[part]).wait()
    for copy in known:
        copy.wait()
    out = substitute(1, PB, (0,), factor_ref, solved_ref, hi_ref, lo_ref, hi_out, lo_out, out_sems)
    head_ref[...] = solved_ref[pl.ds(pl.multiple_of(lax.axis_index("row") * 32, 32), 32), :]
    for copy in out:
        copy.wait()


def solve_second(pieces, hi, lo, second):
    vmem, whole = pl.BlockSpec(memory_space=pltpu.VMEM), pl.BlockSpec(memory_space=pltpu.HBM)
    return pl.pallas_call(
        solve_second_kernel,
        out_shape=(
            jax.ShapeDtypeStruct((32, NE), F32),
            jax.ShapeDtypeStruct((PB, NE), BF16),
            jax.ShapeDtypeStruct((PB, NE), BF16),
        ),
        in_specs=[whole] * 13,
        out_specs=(vmem, whole, whole),
        scratch_shapes=[
            pltpu.VMEM((2, 8, PB, 128), F32),
            pltpu.VMEM((PB, NE), F32),
            pltpu.VMEM((2 * PB, NE), BF16),
            pltpu.VMEM((2 * PB, NE), BF16),
            pltpu.SemaphoreType.DMA((5,)),
            pltpu.SemaphoreType.DMA((2, 4)),
        ],
        compiler_params=pltpu.CompilerParams(vmem_limit_bytes=60 << 20),
        cost_estimate=pl.CostEstimate(flops=20 << 30, bytes_accessed=16 << 20, transcendentals=0),
        name="solve_second",
    )(*pieces, hi, lo, second)


def tail_kernel(points_ref, eval_ref, scale_ref, out_ref):
    right = features(eval_ref[...], scale_ref[...], True)
    out_ref[...] = matern(features(points_ref[...], scale_ref[...], False), right)


def tail_block(points, evals, scale):
    vmem = pl.BlockSpec(memory_space=pltpu.VMEM)
    return pl.pallas_call(
        tail_kernel,
        grid=(4,),
        out_shape=jax.ShapeDtypeStruct((1024, NE), F32),
        in_specs=[pl.BlockSpec((8, 256), lambda i: (0, i)), vmem, vmem],
        out_specs=pl.BlockSpec((256, NE), lambda i: (i, 0)),
        cost_estimate=pl.CostEstimate(flops=1 << 28, bytes_accessed=4 << 20, transcendentals=2 << 20),
        name="tail_block",
    )(points, evals, scale)


def update_kernel(tail_in, a_in, hi_one, lo_one, hi_two, lo_two, out_ref, a_ref, hi_ref, lo_ref, rows_ref, sems, out_sems):
    fetches = []

    def fetch(source, target):
        copy = pltpu.make_async_copy(source, target, sems.at[len(fetches)])
        copy.start()
        fetches.append(copy)
        return copy

    def rows(b):
        return slice(b * 256, b * 256 + 256)

    def part(b):
        return [fetch(a_in.at[:, :, rows(b)], a_ref.at[:, :, rows(b)]), fetch(tail_in.at[rows(b)], rows_ref.at[rows(b)])]

    def known(q):
        at = slice(q * PB, q * PB + PB)
        solved = ((hi_one, lo_one), (hi_two, lo_two))[q]
        return [fetch(i, o.at[at]) for i, o in zip(solved, (hi_ref, lo_ref))]

    arrive = [part(0)]
    solved = [known(0), known(1)]
    arrive += [part(b) for b in range(1, 4)]
    out = []
    for b in range(4):
        for copy in arrive[b]:
            copy.wait()
        for q in range(2):
            if b == 0:
                for copy in solved[q]:
                    copy.wait()
            left = jnp.concatenate([a_ref[z, q, rows(b), :] for z in range(8)], 1)
            at = slice(q * PB, q * PB + PB)
            rows_ref[rows(b)] = rows_ref[rows(b)] - mm3(split2(left), (hi_ref[at, :], lo_ref[at, :]))
        out.append(pltpu.make_async_copy(rows_ref.at[rows(b)], out_ref.at[rows(b)], out_sems.at[b]))
        out[b].start()
    for copy in out:
        copy.wait()


def update(tail, a, one, two):
    whole = pl.BlockSpec(memory_space=pltpu.HBM)
    return pl.pallas_call(
        update_kernel,
        out_shape=jax.ShapeDtypeStruct((1024, NE), F32),
        in_specs=[whole] * 6,
        out_specs=whole,
        scratch_shapes=[
            pltpu.VMEM((8, 2, 1024, 128), F32),
            pltpu.VMEM((2 * PB, NE), BF16),
            pltpu.VMEM((2 * PB, NE), BF16),
            pltpu.VMEM((1024, NE), F32),
            pltpu.SemaphoreType.DMA((12,)),
            pltpu.SemaphoreType.DMA((4,)),
        ],
        compiler_params=pltpu.CompilerParams(vmem_limit_bytes=60 << 20),
        cost_estimate=pl.CostEstimate(flops=12 << 30, bytes_accessed=24 << 20, transcendentals=0),
        name="update_tail",
    )(tail, a, *one, *two)


def hop(v, phase, shift):
    moves = []
    for r in range(32):
        y, x, core = r // 8, (r // 2) % 4, r % 2
        if (core + phase) % 2 == 0:
            x = (x + shift) % 4
        else:
            y = (y + shift) % 4
        moves.append((r, (y * 4 + x) * 2 + core))
    return lax.ppermute(v, "row", moves)


def swap_cores(pieces):
    return [lax.ppermute(v, "row", [(r, r ^ 1) for r in range(32)]) for v in pieces]


def per_device(head_points, tail_points, eval_points, length_scales, head_factor, tail_factor):
    tail_rows = lax.all_gather(tail_factor.transpose(1, 0, 2), "col", axis=0, tiled=False)
    scale = (5.0**0.5 / length_scales)[:, None]
    own = invert_own(head_factor.reshape(2, 64, 128))
    tiles = [own] + [lax.ppermute(own, "col", [(z, (z + d) % 8) for z in range(8)]) for d in range(1, 8)]
    tail = tail_block(tail_points, eval_points, scale)

    points = jnp.pad(head_points.reshape(8, 64), ((0, 0), (0, 64)))
    shard = pack(points, tiles)
    before, after = hop(shard, 0, 1), hop(shard, 0, -1)
    halves = [hop(before[:12], 0, 1), hop(after[12:], 0, -1)]
    line = jnp.stack([shard, before, after, jnp.concatenate(halves, 0)])

    near, far = line[:, :9], line[:, 9:]
    near_before, near_after = hop(near, 1, 1), hop(near, 1, -1)
    far_before, far_after = hop(far, 1, 1), hop(far, 1, -1)
    near = [near, near_before, near_after, hop(near_before, 1, 1)]
    near = near + swap_cores(near)
    near, far_before, far_after = lax.optimization_barrier((near, far_before, far_after))
    far = [far, far_before, far_after, hop(far_before[:2], 1, 1), hop(far_after[2:], 1, -1)]

    head_one, hi_one, lo_one, second = solve_first(near, scale, eval_points)
    head_two, hi_two, lo_two = solve_second(far + swap_cores(far), hi_one, lo_one, second)
    tail = update(tail, tail_rows, (hi_one, lo_one), (hi_two, lo_two))
    return jnp.stack([head_one, head_two]), tail


def solution(mesh):
    placed = (
        P(None, None, "row"),
        P(None, "row"),
        P(None, "col"),
        P(),
        P(None, "row", None, "col"),
        P("row", None, "col"),
    )
    return jax.shard_map(
        per_device,
        mesh=mesh,
        in_specs=placed,
        out_specs=(P(None, "row", "col"), P("row", "col")),
        check_vma=False,
    )
```

```python
import jax
import jax.numpy as jnp
from jax import lax
from jax.experimental import pallas as pl
from jax.experimental.pallas import tpu as pltpu
from jax.sharding import PartitionSpec as P

F32, BF16 = jnp.float32, jnp.bfloat16
PB, NE = 1024, 1024
HALVES = 2
OFFSETS = (0, -1, 1, 2)


def split2(v):
    hi = v.astype(BF16)
    return hi, (v - hi.astype(F32)).astype(BF16)


def split3(v):
    a = v.astype(BF16)
    rest = v - a.astype(F32)
    b = rest.astype(BF16)
    return a, b, (rest - b.astype(F32)).astype(BF16)


def mm(a, b):
    return jnp.dot(a, b, preferred_element_type=F32)


def mm3(a, b):
    return mm(a[0], b[0]) + (mm(a[0], b[1]) + mm(a[1], b[0]))


def features(points, scale, right):
    u = (points - 0.5) * scale
    n = u.shape[1]
    norm = jnp.sum(u * u, axis=0, keepdims=True)
    one, none = jnp.ones((1, n), F32), jnp.zeros((6, n), F32)
    rest = jnp.zeros((32, n), BF16)
    if right:
        a, b, c = split3(jnp.concatenate([-2.0 * u, one, norm, none], 0))
        return jnp.concatenate([a, b, a, c, b, a, rest], 0)
    a, b, c = split3(jnp.concatenate([u, norm, one, none], 0))
    return jnp.concatenate([a, a, b, a, b, c, rest], 0)


def matern(left, right):
    total = lax.dot_general(left, right, (((0,), (0,)), ((), ())), preferred_element_type=F32)
    total = jnp.maximum(total, 0.0)
    scaled = jnp.sqrt(total)
    return (1.0 + scaled + total * (1.0 / 3.0)) * jnp.exp(-scaled)


def invert_own_kernel(tiles_ref, out_ref):
    r, z = lax.axis_index("row"), lax.axis_index("col")
    start = (r % 4) * 32
    mine = z == r // 4
    row = lax.broadcasted_iota(jnp.int32, (32, 128), 0)
    lane = lax.broadcasted_iota(jnp.int32, (32, 128), 1)
    inside = (lane >= start) & (lane < start + 32) & mine
    work = []
    for panel in range(2):
        tile = tiles_ref[panel, pl.ds(panel, 32, stride=2), :]
        block = pltpu.roll(tile, (128 - start) % 128, 1)
        diagonal = jnp.sum(jnp.where(lane == row, block, 0.0), axis=1, keepdims=True)
        scale = 1.0 / diagonal
        work.append([tile, block * scale, jnp.where(lane == row, scale, 0.0)])
    for k in range(31):
        for item in work:
            below = jnp.where(row > k, item[1][:, k : k + 1], 0.0)
            item[2] = item[2] - below * item[2][k : k + 1, :]
    done = [jnp.where(inside, pltpu.roll(x, start, 1), tile) for tile, _, x in work]
    for copy in range(8):
        out_ref[copy, 0:32, :] = done[0]
        out_ref[copy, 32:64, :] = tiles_ref[1, pl.ds(0, 32, stride=2), :]
        out_ref[copy, 64:96, :] = done[1]


def invert_own(tiles):
    vmem = pl.BlockSpec(memory_space=pltpu.VMEM)
    return pl.pallas_call(
        invert_own_kernel,
        out_shape=jax.ShapeDtypeStruct((8, 96, 128), F32),
        in_specs=[vmem],
        out_specs=vmem,
        cost_estimate=pl.CostEstimate(flops=1 << 20, bytes_accessed=1 << 17, transcendentals=0),
        name="invert_own",
    )(tiles)


def block_inverses(blocks):
    row = lax.broadcasted_iota(jnp.int32, (256, 256), 0)
    column = lax.broadcasted_iota(jnp.int32, (256, 256), 1)
    inverse = [jnp.where(row // 32 == column // 32, w, 0.0) for w in blocks]
    for size in (32, 64, 128):
        below = (row // (2 * size) == column // (2 * size)) & (row // size % 2 == 1) & (column // size % 2 == 0)
        inner = [mm3(split2(jnp.where(below, w, 0.0)), split2(d)) for w, d in zip(blocks, inverse)]
        inverse = [d - mm3(split2(d), split2(t)) for d, t in zip(inverse, inner)]
    return [split2(d) for d in inverse]


def source_row(other, k, m):
    r = lax.axis_index("row")
    y, x, source = r // 8, (r // 2) % 4, (r % 2 + other) % 2
    first, second = OFFSETS[m], OFFSETS[k]
    yy = (y + 4 + jnp.where(source == 0, second, first)) % 4
    xx = (x + 4 + jnp.where(source == 0, first, second)) % 4
    return pl.multiple_of(32 * ((yy * 4 + xx) * 2 + source), 32)


def entries(pieces):
    count = len(pieces) // 2
    for n, piece in enumerate(pieces):
        other, k = n // count, n % count
        for m in range(piece.shape[0]):
            yield piece, m, other, min(k, 3), m + (2 if k == 4 else 0)


def substitute(part, at, before, factor_ref, solved_ref, hi_ref, lo_ref, outs=(), sems=None):
    def tiles(p, rows, count):
        return [factor_ref[p, n, rows, :] for n in range(count)]

    blocks = [slice(i * 256, i * 256 + 256) for i in range(4)]
    inverse = block_inverses([jnp.concatenate(tiles(part, rows, 2 * i + 2)[2 * i :], 1) for i, rows in enumerate(blocks)])
    halves = [slice(h * NE // HALVES, (h + 1) * NE // HALVES) for h in range(HALVES)]
    out = []
    for i, rows in enumerate(blocks):
        left = [t for p in before for t in tiles(p, rows, 8)] + tiles(part, rows, 2 * i)
        total = [solved_ref[rows, cols] for cols in halves]
        here = at + i * 256
        if left:
            left = split2(jnp.concatenate(left, 1))
            total = [t - mm3(left, (hi_ref[0:here, cols], lo_ref[0:here, cols])) for t, cols in zip(total, halves)]
        total = [mm3(inverse[i], split2(t)) for t in total]
        for t, cols in zip(total, halves):
            solved_ref[rows, cols] = t
            hi_ref[here : here + 256, cols], lo_ref[here : here + 256, cols] = split2(t)
        for n, (ref, whole) in enumerate(zip((hi_ref, lo_ref), outs)):
            out.append(pltpu.make_async_copy(ref.at[here : here + 256], whole.at[rows], sems.at[n, i]))
            out[-1].start()
    return out


def solve_first_kernel(*refs):
    pieces, (scale_ref, eval_ref, head_ref, hi_out, lo_out, second_out) = refs[:10], refs[10:16]
    points_ref, factor_ref, solved_ref, second_ref, hi_ref, lo_ref, sems, out_sems = refs[16:]
    near = []
    for n, piece in enumerate(pieces):
        target = points_ref.at[n // 5, min(n % 5, 3)]
        if n % 5 >= 3:
            target = target.at[(n % 5 - 3) * 2 : (n % 5 - 3) * 2 + 2]
        near.append(pltpu.make_async_copy(piece.at[:, 0, 0:8], target, sems.at[n]))
        near[-1].start()
    rows = []
    for piece, m, other, k, entry in entries(pieces):
        row = source_row(other, k, entry)
        rows.append(row)
        pltpu.make_async_copy(piece.at[m, 1:9], factor_ref.at[0, :, pl.ds(row, 32)], sems.at[10]).start()
    right = features(eval_ref[...], scale_ref[...], True)
    for copy in near:
        copy.wait()
    for panel, target in ((0, solved_ref), (1, second_ref)):
        for n in range(0, 32, 8):
            points = [points_ref[e // 16, e // 4 % 4, e % 4, :, panel * 32 : panel * 32 + 32] for e in range(n, n + 8)]
            values = matern(features(jnp.concatenate(points, 1), scale_ref[...], False), right)
            for j in range(8):
                target[pl.ds(rows[n + j], 32), :] = values[j * 32 : j * 32 + 32, :]
    second = pltpu.make_async_copy(second_ref, second_out, sems.at[11])
    second.start()
    pltpu.make_async_copy(factor_ref, factor_ref, sems.at[10]).wait()
    out = substitute(0, 0, (), factor_ref, solved_ref, hi_ref, lo_ref, (hi_out, lo_out), out_sems)
    head_ref[...] = solved_ref[pl.ds(pl.multiple_of(lax.axis_index("row") * 32, 32), 32), :]
    for copy in out:
        copy.wait()
    second.wait()


def solve_first(pieces, scale, evals):
    vmem, whole = pl.BlockSpec(memory_space=pltpu.VMEM), pl.BlockSpec(memory_space=pltpu.HBM)
    return pl.pallas_call(
        solve_first_kernel,
        out_shape=(
            jax.ShapeDtypeStruct((32, NE), F32),
            jax.ShapeDtypeStruct((PB, NE), BF16),
            jax.ShapeDtypeStruct((PB, NE), BF16),
            jax.ShapeDtypeStruct((PB, NE), F32),
        ),
        in_specs=[whole] * 10 + [vmem] * 2,
        out_specs=(vmem, whole, whole, whole),
        scratch_shapes=[
            pltpu.VMEM((2, 4, 4, 8, 128), F32),
            pltpu.VMEM((1, 8, PB, 128), F32),
            pltpu.VMEM((PB, NE), F32),
            pltpu.VMEM((PB, NE), F32),
            pltpu.VMEM((PB, NE), BF16),
            pltpu.VMEM((PB, NE), BF16),
            pltpu.SemaphoreType.DMA((12,)),
            pltpu.SemaphoreType.DMA((2, 4)),
        ],
        compiler_params=pltpu.CompilerParams(vmem_limit_bytes=60 << 20),
        cost_estimate=pl.CostEstimate(flops=9 << 30, bytes_accessed=8 << 20, transcendentals=4 << 20),
        name="solve_first",
    )(*pieces, scale, evals)


def tail_kernel(points_ref, eval_ref, scale_ref, out_ref):
    right = features(eval_ref[...], scale_ref[...], True)
    out_ref[...] = matern(features(points_ref[...], scale_ref[...], False), right)


def tail_block(points, evals, scale):
    vmem = pl.BlockSpec(memory_space=pltpu.VMEM)
    return pl.pallas_call(
        tail_kernel,
        grid=(4,),
        out_shape=jax.ShapeDtypeStruct((1024, NE), F32),
        in_specs=[pl.BlockSpec((8, 256), lambda i: (0, i)), vmem, vmem],
        out_specs=pl.BlockSpec((256, NE), lambda i: (i, 0)),
        cost_estimate=pl.CostEstimate(flops=1 << 28, bytes_accessed=4 << 20, transcendentals=2 << 20),
        name="tail_block",
    )(points, evals, scale)


def finish_kernel(*refs):
    pieces, (hi_in, lo_in, second_in, head_one_ref, tail_in, a_in, head_ref, out_ref) = refs[:10], refs[10:18]
    factor_ref, solved_ref, hi_ref, lo_ref, a_ref, rows_ref, sems, tail_sems, out_sems = refs[18:]
    for part in (1, 0):
        for piece, m, other, k, entry in entries(pieces):
            target = factor_ref.at[part, :, pl.ds(source_row(other, k, entry), 32)]
            pltpu.make_async_copy(piece.at[m, part * 8 + 9 : part * 8 + 17], target, sems.at[part]).start()
    known = [
        pltpu.make_async_copy(hi_in, hi_ref.at[0:PB], sems.at[2]),
        pltpu.make_async_copy(lo_in, lo_ref.at[0:PB], sems.at[3]),
        pltpu.make_async_copy(second_in, solved_ref, sems.at[4]),
    ]
    arrive = []
    for b in range(4):
        rows, pairs = slice(b * 256, b * 256 + 256), slice(b * 512, b * 512 + 512)
        arrive.append(
            [
                pltpu.make_async_copy(a_in.at[:, pairs], a_ref.at[:, pairs], tail_sems.at[0, b]),
                pltpu.make_async_copy(tail_in.at[rows], rows_ref.at[rows], tail_sems.at[1, b]),
            ]
        )
    for copy in known + [c for pair in arrive for c in pair]:
        copy.start()
    for part in (1, 0):
        pltpu.make_async_copy(factor_ref.at[part], factor_ref.at[part], sems.at[part]).wait()
    for copy in known:
        copy.wait()
    substitute(1, PB, (0,), factor_ref, solved_ref, hi_ref, lo_ref)
    head_ref[0] = head_one_ref[...]
    head_ref[1] = solved_ref[pl.ds(pl.multiple_of(lax.axis_index("row") * 32, 32), 32), :]
    out = []
    for b in range(4):
        rows = slice(b * 256, b * 256 + 256)
        for copy in arrive[b]:
            copy.wait()
        left = [a_ref[z, pl.ds(b * 512 + q, 256, stride=2), :] for q in range(2) for z in range(8)]
        left = split2(jnp.concatenate(left, 1))
        rows_ref[rows] = rows_ref[rows] - mm3(left, (hi_ref[...], lo_ref[...]))
        out.append(pltpu.make_async_copy(rows_ref.at[rows], out_ref.at[rows], out_sems.at[b]))
        out[b].start()
    for copy in out:
        copy.wait()


def finish(pieces, hi, lo, second, head_one, tail, a):
    vmem, whole = pl.BlockSpec(memory_space=pltpu.VMEM), pl.BlockSpec(memory_space=pltpu.HBM)
    return pl.pallas_call(
        finish_kernel,
        out_shape=(jax.ShapeDtypeStruct((2, 32, NE), F32), jax.ShapeDtypeStruct((1024, NE), F32)),
        in_specs=[whole] * 13 + [vmem, whole, whole],
        out_specs=(vmem, whole),
        scratch_shapes=[
            pltpu.VMEM((2, 8, PB, 128), F32),
            pltpu.VMEM((PB, NE), F32),
            pltpu.VMEM((2 * PB, NE), BF16),
            pltpu.VMEM((2 * PB, NE), BF16),
            pltpu.VMEM((8, 2048, 128), F32),
            pltpu.VMEM((1024, NE), F32),
            pltpu.SemaphoreType.DMA((5,)),
            pltpu.SemaphoreType.DMA((2, 4)),
            pltpu.SemaphoreType.DMA((4,)),
        ],
        compiler_params=pltpu.CompilerParams(vmem_limit_bytes=60 << 20),
        cost_estimate=pl.CostEstimate(flops=32 << 30, bytes_accessed=36 << 20, transcendentals=0),
        name="finish",
    )(*pieces, hi, lo, second, head_one, tail, a)


def hop(v, phase, shift):
    moves = []
    for r in range(32):
        y, x, core = r // 8, (r // 2) % 4, r % 2
        if (core + phase) % 2 == 0:
            x = (x + shift) % 4
        else:
            y = (y + shift) % 4
        moves.append((r, (y * 4 + x) * 2 + core))
    return lax.ppermute(v, "row", moves)


def swap_cores(pieces):
    return [lax.ppermute(v, "row", [(r, r ^ 1) for r in range(32)]) for v in pieces]


def per_device(head_points, tail_points, eval_points, length_scales, head_factor, tail_factor):
    tail_rows = lax.all_gather(tail_factor, "col", axis=0, tiled=False).reshape(8, 2048, 128)
    scale = (5.0**0.5 / length_scales)[:, None]
    spread = lax.all_to_all(invert_own(head_factor.reshape(2, 64, 128)), "col", 0, 0)
    tail = tail_block(tail_points, eval_points, scale)
    spread, tail = lax.optimization_barrier((spread, tail))

    points = jnp.pad(head_points.reshape(8, 64), ((0, 24), (0, 64)))[None]
    blocks = spread.reshape(8, 3, 32, 128).transpose(1, 0, 2, 3).reshape(24, 32, 128)
    shard = jnp.concatenate([points, blocks], 0)
    before, after = hop(shard, 0, 1), hop(shard, 0, -1)
    halves = [hop(before[:12], 0, 1), hop(after[12:], 0, -1)]
    line = jnp.stack([shard, before, after, jnp.concatenate(halves, 0)])
    before, after = hop(line, 1, 1), hop(line, 1, -1)
    plane = [line, before, after, hop(before[:2], 1, 1), hop(after[2:], 1, -1)]
    pieces = plane + swap_cores(plane)

    head_one, hi, lo, second = solve_first(pieces, scale, eval_points)
    return finish(pieces, hi, lo, second, head_one, tail, tail_rows)


def solution(mesh):
    placed = (
        P(None, None, "row"),
        P(None, "row"),
        P(None, "col"),
        P(),
        P(None, "row", None, "col"),
        P("row", None, "col"),
    )
    return jax.shard_map(
        per_device,
        mesh=mesh,
        in_specs=placed,
        out_specs=(P(None, "row", "col"), P("row", "col")),
        check_vma=False,
    )
```

```python
import jax
import jax.numpy as jnp
from jax import lax
from jax.experimental import pallas as pl
from jax.experimental.pallas import tpu as pltpu
from jax.sharding import PartitionSpec as P

F32, BF16 = jnp.float32, jnp.bfloat16
PB, NE = 1024, 1024
HALVES = 2
OFFSETS = (0, -1, 1, 2)
SHARD = 3 * 8 * 32 + 8


def split2(v):
    hi = v.astype(BF16)
    return hi, (v - hi.astype(F32)).astype(BF16)


def split3(v):
    a = v.astype(BF16)
    rest = v - a.astype(F32)
    b = rest.astype(BF16)
    return a, b, (rest - b.astype(F32)).astype(BF16)


def mm(a, b):
    return jnp.dot(a, b, preferred_element_type=F32)


def mm3(a, b):
    return mm(jnp.concatenate([a[0], a[0], a[1]], 1), jnp.concatenate([b[0], b[1], b[0]], 0))


def features(points, scale, right):
    u = (points - 0.5) * scale
    n = u.shape[1]
    norm = jnp.sum(u * u, axis=0, keepdims=True)
    one, none = jnp.ones((1, n), F32), jnp.zeros((6, n), F32)
    rest = jnp.zeros((32, n), BF16)
    if right:
        a, b, c = split3(jnp.concatenate([-2.0 * u, one, norm, none], 0))
        return jnp.concatenate([a, b, a, c, b, a, rest], 0)
    a, b, c = split3(jnp.concatenate([u, norm, one, none], 0))
    return jnp.concatenate([a, a, b, a, b, c, rest], 0)


def matern(left, right):
    total = lax.dot_general(left, right, (((0,), (0,)), ((), ())), preferred_element_type=F32)
    total = jnp.maximum(total, 0.0)
    scaled = jnp.sqrt(total)
    return (1.0 + scaled + total * (1.0 / 3.0)) * jnp.exp(-scaled)


def invert_own_kernel(tiles_ref, out_ref):
    r, z = lax.axis_index("row"), lax.axis_index("col")
    start = (r % 4) * 32
    mine = z == r // 4
    row = lax.broadcasted_iota(jnp.int32, (32, 128), 0)
    lane = lax.broadcasted_iota(jnp.int32, (32, 128), 1)
    inside = (lane >= start) & (lane < start + 32) & mine
    work = []
    for panel in range(2):
        tile = tiles_ref[panel, pl.ds(panel, 32, stride=2), :]
        block = pltpu.roll(tile, (128 - start) % 128, 1)
        diagonal = jnp.sum(jnp.where(lane == row, block, 0.0), axis=1, keepdims=True)
        scale = 1.0 / diagonal
        work.append([tile, block * scale, jnp.where(lane == row, scale, 0.0)])
    for k in range(31):
        for item in work:
            below = jnp.where(row > k, item[1][:, k : k + 1], 0.0)
            item[2] = item[2] - below * item[2][k : k + 1, :]
    done = [jnp.where(inside, pltpu.roll(x, start, 1), tile) for tile, _, x in work]
    for copy in range(8):
        out_ref[copy, 0:32, :] = done[0]
        out_ref[copy, 32:64, :] = tiles_ref[1, pl.ds(0, 32, stride=2), :]
        out_ref[copy, 64:96, :] = done[1]


def invert_own(tiles):
    vmem = pl.BlockSpec(memory_space=pltpu.VMEM)
    return pl.pallas_call(
        invert_own_kernel,
        out_shape=jax.ShapeDtypeStruct((8, 96, 128), F32),
        in_specs=[vmem],
        out_specs=vmem,
        cost_estimate=pl.CostEstimate(flops=1 << 20, bytes_accessed=1 << 19, transcendentals=0),
        name="invert_own",
    )(tiles)


def block_inverses(factor):
    row = lax.broadcasted_iota(jnp.int32, (256, 256), 0)
    column = lax.broadcasted_iota(jnp.int32, (256, 256), 1)
    whole = [
        jnp.concatenate([factor[2 * i, i * 256 : i * 256 + 256, :], factor[2 * i + 1, i * 256 : i * 256 + 256, :]], 1)
        for i in range(4)
    ]
    inverse = [jnp.where(row // 32 == column // 32, w, 0.0) for w in whole]
    for size in (32, 64, 128):
        below = (row // (2 * size) == column // (2 * size)) & (row // size % 2 == 1) & (column // size % 2 == 0)
        inner = [mm3(split2(jnp.where(below, w, 0.0)), split2(d)) for w, d in zip(whole, inverse)]
        inverse = [d - mm3(split2(d), split2(t)) for d, t in zip(inverse, inner)]
    return inverse


def solve_kernel(*refs):
    pieces, (scale_ref, eval_ref, head_ref, hi_out, lo_out) = refs[:10], refs[10:15]
    stage_ref, factor_ref, solved_ref, hi_ref, lo_ref, sems, out_sems = refs[15:]
    r = lax.axis_index("row")
    y, x, core = r // 8, (r // 2) % 4, r % 2
    early, late = [], []
    for n, piece in enumerate(pieces):
        at = stage_ref.at[n // 5, min(n % 5, 3)]
        if n % 5 >= 3:
            at = at.at[(n % 5 - 3) * 2 : (n % 5 - 3) * 2 + 2]
        early.append(pltpu.make_async_copy(piece.at[:, 0:264], at.at[:, 0:264], sems.at[0, n]))
        late.append(pltpu.make_async_copy(piece.at[:, 264:SHARD], at.at[:, 264:SHARD], sems.at[1, n]))
    for copy in early:
        copy.start()
    sources = []
    for other in range(2):
        source = (core + other) % 2
        for k in range(4):
            for m in range(4):
                first, second = OFFSETS[m], OFFSETS[k]
                yy = (y + 4 + jnp.where(source == 0, second, first)) % 4
                xx = (x + 4 + jnp.where(source == 0, first, second)) % 4
                sources.append((stage_ref.at[other, k, m], pl.multiple_of(32 * ((yy * 4 + xx) * 2 + source), 32)))
    right = features(eval_ref[...], scale_ref[...], True)

    def place(part, at):
        for stage, row in sources:
            for z in range(8):
                factor_ref[part, z, pl.ds(row, 32), :] = stage[at + z * 32 : at + z * 32 + 32, :]

    for copy in early:
        copy.wait()
    for copy in late:
        copy.start()
    place(0, 8)
    for panel in range(2):
        for n in range(0, 32, 8):
            points = jnp.concatenate([s[0:8, panel * 32 : panel * 32 + 32] for s, _ in sources[n : n + 8]], 1)
            values = matern(features(points, scale_ref[...], False), right)
            for j, (_, row) in enumerate(sources[n : n + 8]):
                solved_ref[panel, pl.ds(row, 32), :] = values[j * 32 : j * 32 + 32, :]

    out = []
    for panel in range(2):
        if panel == 1:
            for copy in late:
                copy.wait()
            place(1, 264)
            place(2, 520)
        inverse = [split2(v) for v in block_inverses(factor_ref.at[2 * panel])]
        for i in range(4):
            rows = slice(i * 256, i * 256 + 256)
            left = [factor_ref[1, z, rows, :] for z in range(8)] if panel else []
            left += [factor_ref[2 * panel, z, rows, :] for z in range(2 * i)]
            at = panel * PB + i * 256
            left = split2(jnp.concatenate(left, 1)) if left else None
            halves = [slice(h * NE // HALVES, (h + 1) * NE // HALVES) for h in range(HALVES)]
            total = [solved_ref[panel, rows, cols] for cols in halves]
            if left is not None:
                total = [t - mm3(left, (hi_ref[0:at, cols], lo_ref[0:at, cols])) for t, cols in zip(total, halves)]
            total = [mm3(inverse[i], split2(t)) for t in total]
            for t, cols in zip(total, halves):
                solved_ref[panel, rows, cols] = t
                hi_ref[at : at + 256, cols], lo_ref[at : at + 256, cols] = split2(t)
            for n, (ref, whole) in enumerate(((hi_ref, hi_out), (lo_ref, lo_out))):
                sem = out_sems.at[n, panel * 4 + i]
                out.append(pltpu.make_async_copy(ref.at[at : at + 256], whole.at[at : at + 256], sem))
                out[-1].start()
    own = pl.multiple_of(r * 32, 32)
    for panel in range(2):
        head_ref[panel] = solved_ref[panel, pl.ds(own, 32), :]
    for copy in out:
        copy.wait()


def solve(pieces, scale, evals):
    vmem, whole = pl.BlockSpec(memory_space=pltpu.VMEM), pl.BlockSpec(memory_space=pl.ANY)
    return pl.pallas_call(
        solve_kernel,
        out_shape=(
            jax.ShapeDtypeStruct((2, 32, NE), F32),
            jax.ShapeDtypeStruct((2 * PB, NE), BF16),
            jax.ShapeDtypeStruct((2 * PB, NE), BF16),
        ),
        in_specs=[whole] * 10 + [vmem] * 2,
        out_specs=(vmem, whole, whole),
        scratch_shapes=[
            pltpu.VMEM((2, 4, 4, SHARD, 128), F32),
            pltpu.VMEM((3, 8, PB, 128), F32),
            pltpu.VMEM((2, PB, NE), F32),
            pltpu.VMEM((2 * PB, NE), BF16),
            pltpu.VMEM((2 * PB, NE), BF16),
            pltpu.SemaphoreType.DMA((2, 10)),
            pltpu.SemaphoreType.DMA((2, 8)),
        ],
        compiler_params=pltpu.CompilerParams(vmem_limit_bytes=47 << 20),
        cost_estimate=pl.CostEstimate(flops=15 << 30, bytes_accessed=16 << 20, transcendentals=4 << 20),
        name="solve_panels",
    )(*pieces, scale, evals)


def tail_kernel(points_ref, eval_ref, scale_ref, out_ref):
    right = features(eval_ref[...], scale_ref[...], True)
    out_ref[...] = matern(features(points_ref[...], scale_ref[...], False), right)


def tail_block(points, evals, scale):
    vmem = pl.BlockSpec(memory_space=pltpu.VMEM)
    return pl.pallas_call(
        tail_kernel,
        grid=(4,),
        out_shape=jax.ShapeDtypeStruct((1024, NE), F32),
        in_specs=[pl.BlockSpec((8, 256), lambda i: (0, i)), vmem, vmem],
        out_specs=pl.BlockSpec((256, NE), lambda i: (i, 0)),
        cost_estimate=pl.CostEstimate(flops=1 << 28, bytes_accessed=4 << 20, transcendentals=2 << 20),
        name="tail_block",
    )(points, evals, scale)


def update_kernel(tail_in, a_in, hi_in, lo_in, out_ref, a_ref, hi_ref, lo_ref, rows_ref, sems, out_sems):
    fetches = []

    def fetch(source, target):
        copy = pltpu.make_async_copy(source, target, sems.at[len(fetches)])
        copy.start()
        fetches.append(copy)
        return copy

    def rows(b):
        return slice(b * 256, b * 256 + 256)

    def part(b):
        return [fetch(a_in.at[:, :, rows(b)], a_ref.at[:, :, rows(b)]), fetch(tail_in.at[rows(b)], rows_ref.at[rows(b)])]

    def known(q):
        at = slice(q * PB, q * PB + PB)
        return [fetch(i.at[at], o.at[at]) for i, o in ((hi_in, hi_ref), (lo_in, lo_ref))]

    arrive = [part(0)]
    solved = [known(0), known(1)]
    out = []
    for b in range(4):
        for copy in arrive[b]:
            copy.wait()
        for q in range(2):
            if b == 0:
                for copy in solved[q]:
                    copy.wait()
                arrive += [part(n) for n in ((1,), (2, 3))[q]]
            left = jnp.concatenate([a_ref[z, q, rows(b), :] for z in range(8)], 1)
            at = slice(q * PB, q * PB + PB)
            rows_ref[rows(b)] = rows_ref[rows(b)] - mm3(split2(left), (hi_ref[at, :], lo_ref[at, :]))
        out.append(pltpu.make_async_copy(rows_ref.at[rows(b)], out_ref.at[rows(b)], out_sems.at[b]))
        out[b].start()
    for copy in out:
        copy.wait()


def update(tail, a, hi, lo):
    whole = pl.BlockSpec(memory_space=pl.ANY)
    return pl.pallas_call(
        update_kernel,
        out_shape=jax.ShapeDtypeStruct((1024, NE), F32),
        in_specs=[whole] * 4,
        out_specs=whole,
        scratch_shapes=[
            pltpu.VMEM((8, 2, 1024, 128), F32),
            pltpu.VMEM((2 * PB, NE), BF16),
            pltpu.VMEM((2 * PB, NE), BF16),
            pltpu.VMEM((1024, NE), F32),
            pltpu.SemaphoreType.DMA((12,)),
            pltpu.SemaphoreType.DMA((4,)),
        ],
        compiler_params=pltpu.CompilerParams(vmem_limit_bytes=58 << 20),
        cost_estimate=pl.CostEstimate(flops=12 << 30, bytes_accessed=24 << 20, transcendentals=0),
        name="update_tail",
    )(tail, a, hi, lo)


def hop(v, phase, shift):
    moves = []
    for r in range(32):
        y, x, core = r // 8, (r // 2) % 4, r % 2
        if (core + phase) % 2 == 0:
            x = (x + shift) % 4
        else:
            y = (y + shift) % 4
        moves.append((r, (y * 4 + x) * 2 + core))
    return lax.ppermute(v, "row", moves)


def gather_four(v, phase, cut):
    from_before, from_after = hop(v, phase, 1), hop(v, phase, -1)
    two_before = hop(from_before[:cut], phase, 1)
    two_after = hop(from_after[cut:], phase, -1)
    return [v, from_before, from_after, two_before, two_after]


def per_device(head_points, tail_points, eval_points, length_scales, head_factor, tail_factor):
    scale = (5.0**0.5 / length_scales)[:, None]
    tiles = invert_own(head_factor.reshape(2, 64, 128))
    spread = lax.all_to_all(tiles, "col", 0, 0)
    tail = tail_block(tail_points, eval_points, scale)
    spread, tail, tail_factor = lax.optimization_barrier((spread, tail, tail_factor.transpose(1, 0, 2)))
    tail_rows = lax.all_gather(tail_factor, "col", axis=0, tiled=False)
    points = jnp.pad(head_points.reshape(8, 64), ((0, 0), (0, 64)))
    spread = spread.reshape(8, 3, 32, 128).transpose(1, 0, 2, 3).reshape(768, 128)
    shard = jnp.concatenate([points, spread], 0)

    line = gather_four(shard, 0, SHARD // 2 // 8 * 8)
    line = jnp.stack(line[:3] + [jnp.concatenate(line[3:], 0)])
    plane = gather_four(line, 1, 2)
    pieces = plane + [lax.ppermute(v, "row", [(r, r ^ 1) for r in range(32)]) for v in plane]

    head, hi, lo = solve(pieces, scale, eval_points)
    tail = update(tail, tail_rows, hi, lo)
    return head, tail


def solution(mesh):
    placed = (
        P(None, None, "row"),
        P(None, "row"),
        P(None, "col"),
        P(),
        P(None, "row", None, "col"),
        P("row", None, "col"),
    )
    return jax.shard_map(
        per_device,
        mesh=mesh,
        in_specs=placed,
        out_specs=(P(None, "row", "col"), P("row", "col")),
        check_vma=False,
    )
```
